32 devices in a mesh: member: 2 (over x), tile: 16 (over z, y, core).
Axes of the slice: x: 2, y: 2, z: 4, core: 2. Of those that a mesh axis runs over, the one named last changes fastest.
Arguments:
- precip: float32 [1024, 128], P(('member', 'tile')), parts along dimension 0, may hold values from 0.2 to 2
- pet: float32 [1024, 128], P(('member', 'tile')), parts along dimension 0, may hold values from 0.05 to 0.5
- soil_init: float32 [1024, 128], P(('member', 'tile')), parts along dimension 0, may hold values from 0.05 to 0.4
- ksat: float32 [1024, 128], P(('member', 'tile')), parts along dimension 0, may hold values from 0.5 to 3
- land_mask: int32 [1024, 128], P(('member', 'tile')), parts along dimension 0, may hold values 0 or 1
- head_init: float32 [1024, 2048], P(('member', 'tile')), parts along dimension 0, may hold values from 0.2 to 2
- subsurface_init: float32 [1024, 2048], P(('member', 'tile')), parts along dimension 0, may hold values from 0.2 to 2
- conduct: float32 [1024, 2048], P(('member', 'tile')), parts along dimension 0, may hold values from 0.22 to 0.47
- drain_rate: float32 [1024, 2048], P(('member', 'tile')), parts along dimension 0, may hold values from 0.05 to 0.4
- flow_code: int32 [1024, 2048], P(('member', 'tile')), parts along dimension 0, may hold values from 0 to 3
- channel_share: float32 [1024, 2048], P(('member', 'tile')), parts along dimension 0, may hold values from 0.02 to 0.2
- cell_slot: int32 [1024, 2048], P(('member', 'tile')), parts along dimension 0, may hold values from 0 to 1023
- slot_reach: int32 [32768], P(('member', 'tile')), parts along dimension 0, may hold values from 0 to 1023
Outputs:
- soil: float32 [1024, 128], P(('member', 'tile')), parts along dimension 0
- head: float32 [1024, 2048], P(('member', 'tile')), parts along dimension 0
- subsurface: float32 [1024, 2048], P(('member', 'tile')), parts along dimension 0
- reach_inflow: float32 [32768], P(('member', 'tile')), parts along dimension 0
The draws below stay inside these ranges and needn't reach their ends.
There are 2 independent parts, one for each index of `member`. The reference program is written for one: setup_inputs(seed, part) draws one part's arguments, and reference() takes and returns one part's arrays. A program takes and returns all parts, laid end to end along the dimension named above; each array names one. Nothing has to cross between parts.
Inputs may be any that keep to these rules, and one draw needn't show every extreme that they name: `slot_reach`: slot k of a tile holds a reach owned by tile index k // 64.
All inputs are finite; a program needn't handle non-finite values. No bound on the sum of `land_mask` on one device may be relied on, other than what follows from the above.
Results may differ from the reference program's by a relative error of at most 0.00002.
Values sent between devices are 32-bit elements; how exact they have to be, the bound alone decides.
A program may use at most 64 MiB of HBM per device.

```python
import math
import jax
import jax.numpy as jnp

FR_DEV = 32
FC = 2048
ITERS = 6
PER_OWNER = 64
REACH_DEV = 1024
FR = 512
CC = 512
CR = 128
SLOTS = 1024
N_TILE = 16


def set_ends(entries, key, least, largest):
    dims = entries.shape
    spot = [jax.random.randint(jax.random.fold_in(key, axis), (), 0, dims[axis]) for axis in range(len(dims))]
    entries = entries.at[tuple(spot)].set(least)
    longest = dims.index(max(dims))
    spot[longest] = (spot[longest] + 1) % dims[longest]
    return entries.at[tuple(spot)].set(largest)


def shard_levels(stream_key, extent, shards, least, largest):
    gain, own = 1.0, jax.random.fold_in(stream_key, 6)
    for position, blocks in shards:
        steps = jnp.exp(jax.random.uniform(jax.random.fold_in(own, position), (blocks,), jnp.float32, least / len(shards), largest / len(shards)))
        gain = gain * jnp.repeat(steps, extent[position] // blocks).reshape([-1 if axis == position else 1 for axis in range(len(extent))])
    return gain


def setup_inputs(seed: int = 0, part: int = 0) -> dict:
    keys = jax.random.split(jax.random.key(seed), 14)
    part_keys = jax.random.split(jax.random.fold_in(keys[13], part), 14)
    return {
        "precip": jnp.clip(jnp.exp(math.log(2.0) - 2.3025851 * jax.random.uniform(part_keys[0], (CC, CR), jnp.float32) ** shard_levels(part_keys[0], (CC, CR), ((0, 16),), -0.2, 0.2)), 0.2, 2.0),
        "pet": jnp.clip(jnp.exp(math.log(0.5) - 2.3025851 * jax.random.uniform(part_keys[1], (CC, CR), jnp.float32) ** shard_levels(part_keys[1], (CC, CR), ((0, 16),), -0.2, 0.2)), 0.05, 0.5),
        "soil_init": jnp.clip(0.05 + 0.35 * jax.random.uniform(part_keys[2], (CC, CR), jnp.float32) ** shard_levels(part_keys[2], (CC, CR), ((0, 16),), -0.2, 0.2), 0.05, 0.4),
        "ksat": jnp.clip(jnp.exp(math.log(3.0) - 1.7917595 * jax.random.uniform(part_keys[3], (CC, CR), jnp.float32) ** shard_levels(part_keys[3], (CC, CR), ((0, 16),), -0.2, 0.2)), 0.5, 3.0),
        "land_mask": set_ends((jax.random.randint(part_keys[4], (CC, CR), 0, 4) < 3).astype(jnp.int32), jax.random.fold_in(part_keys[4], 1), 0, 1),
        "head_init": jnp.clip(jnp.exp(math.log(2.0) - 2.3025851 * jax.random.uniform(part_keys[5], (FR, FC), jnp.float32) ** shard_levels(part_keys[5], (FR, FC), ((0, 16),), -0.2, 0.2)), 0.2, 2.0),
        "subsurface_init": jnp.clip(jnp.exp(math.log(2.0) - 2.3025851 * jax.random.uniform(part_keys[6], (FR, FC), jnp.float32) ** shard_levels(part_keys[6], (FR, FC), ((0, 16),), -0.2, 0.2)), 0.2, 2.0),
        "conduct": jnp.clip(jnp.exp(math.log(0.47) - 0.75910515 * jax.random.uniform(part_keys[7], (FR, FC), jnp.float32) ** shard_levels(part_keys[7], (FR, FC), ((0, 16),), -0.2, 0.2)), 0.22, 0.47),
        "drain_rate": jnp.clip(jnp.exp(math.log(0.4) - 2.0794415 * jax.random.uniform(part_keys[8], (FR, FC), jnp.float32) ** shard_levels(part_keys[8], (FR, FC), ((0, 16),), -0.2, 0.2)), 0.05, 0.4),
        "flow_code": set_ends(jax.random.randint(part_keys[9], (FR, FC), 0, 4), jax.random.fold_in(part_keys[9], 1), 0, 3).astype(jnp.int32),
        "channel_share": jnp.clip(0.02 + 0.18 * jax.random.uniform(part_keys[10], (FR, FC), jnp.float32) ** shard_levels(part_keys[10], (FR, FC), ((0, 16),), -0.2, 0.2), 0.02, 0.2),
        "cell_slot": set_ends(jax.random.randint(part_keys[11], (FR, FC), 0, SLOTS), jax.random.fold_in(part_keys[11], 1), 0, SLOTS - 1).astype(jnp.int32),
        "slot_reach": set_ends(jax.random.randint(part_keys[12], (N_TILE * SLOTS,), 0, REACH_DEV), jax.random.fold_in(part_keys[12], 1), 0, REACH_DEV - 1).astype(jnp.int32),
    }


def land_step(precip, pet, soil_init, ksat, land_mask):
    mask = land_mask.astype(jnp.float32)
    wet = 2.0 * soil_init
    cap = ksat * (1.0 - wet)
    runoff = mask * precip * precip / (precip + cap)
    drainage = 0.25 * mask * ksat * wet ** 4
    evap = mask * pet * wet
    soil = soil_init + 0.1 * (mask * precip - runoff - drainage - evap)
    return soil, runoff, drainage


def advance(state, statics):
    h = state[0]
    s = state[1]
    g, down, up, right, left = statics[0], statics[1], statics[2], statics[3], statics[4]
    hc = h[1:-1]
    gc = g[1:-1]
    sc = s[1:-1]
    hs = jnp.pad(hc, ((0, 0), (1, 1)))
    gs = jnp.pad(gc, ((0, 0), (1, 1)))
    flux = g[:-2] * (h[:-2] - hc) + g[2:] * (h[2:] - hc)
    flux = flux + gs[:, :-2] * (hs[:, :-2] - hc) + gs[:, 2:] * (hs[:, 2:] - hc)
    h_new = hc + gc * flux
    moving_right = jnp.pad((right * s)[1:-1], ((0, 0), (1, 1)))
    moving_left = jnp.pad((left * s)[1:-1], ((0, 0), (1, 1)))
    incoming = (down * s)[:-2] + (up * s)[2:] + moving_right[:, :-2] + moving_left[:, 2:]
    outgoing = (down + up + right + left)[1:-1]
    s_new = sc - outgoing * sc + incoming
    return jnp.stack([h_new, s_new])


def make_statics(conduct, drain_rate, flow_code):
    parts = [conduct]
    for code in range(4):
        parts.append(drain_rate * (flow_code == code).astype(jnp.float32))
    return jnp.stack(parts)


def reference(precip, pet, soil_init, ksat, land_mask, head_init, subsurface_init, conduct, drain_rate, flow_code, channel_share, cell_slot, slot_reach):
    soil, runoff, drainage = land_step(precip, pet, soil_init, ksat, land_mask)
    fine = jnp.stack([runoff.T, drainage.T])
    fine = jnp.repeat(jnp.repeat(fine, 4, axis=1), 4, axis=2)
    state = jnp.stack([head_init + fine[0], subsurface_init + fine[1]])
    statics = jnp.pad(make_statics(conduct, drain_rate, flow_code), ((0, 0), (1, 1), (0, 0)))
    for step in range(ITERS):
        state = advance(jnp.pad(state, ((0, 0), (1, 1), (0, 0))), statics)
    h = state[0]
    inflow = channel_share * h
    head = h - inflow
    rows = jnp.arange(FR, dtype=jnp.int32) // FR_DEV
    slots = PER_OWNER * N_TILE
    place = slot_reach[(rows[:, None] * slots + cell_slot).astype(jnp.int32)]
    reach_id = (cell_slot // PER_OWNER) * REACH_DEV + place
    reach_inflow = jax.ops.segment_sum(inflow.ravel(), reach_id.ravel().astype(jnp.int32), num_segments=REACH_DEV * N_TILE)
    return soil, head, state[1], reach_inflow
```

```python
import functools

import jax
import jax.numpy as jnp
from jax import lax
from jax.experimental import pallas as pl
from jax.experimental.pallas import tpu as pltpu
from jax.sharding import PartitionSpec as P

ITERS = 6
HALO = 8
LANES = 128
MESH = pl.DeviceIdType.MESH
NT = (((1,), (1,)), ((), ()))


def parts_of(x, count):
    parts = []
    for _ in range(count):
        part = x.astype(jnp.bfloat16)
        parts.append(part)
        x = x - part.astype(jnp.float32)
    return parts


def kernel(
    n,
    precip,
    pet,
    soil_init,
    ksat,
    land_mask,
    head_init,
    subsurface_init,
    conduct,
    drain_rate,
    flow_code,
    channel_share,
    cell_slot,
    slot_reach,
    soil_out,
    head_out,
    sub_out,
    reach_out,
    land_in,
    mask_in,
    soil_v,
    pack,
    land_send,
    land_recv,
    wide,
    h,
    s,
    g,
    d,
    code,
    keep_h,
    keep_s,
    from_up,
    from_down,
    from_left,
    from_right,
    share_v,
    slot_v,
    inflow,
    head_v,
    sums_send,
    sums_recv,
    places,
    spots,
    reach_v,
    land_sem,
    own_sem,
    halo_send,
    halo_recv,
    a2a_send,
    a2a_recv,
    out_sem,
):
    me = lax.axis_index("tile")
    cols, land_rows = precip.shape
    rows, width = head_init.shape
    full = rows + 2 * HALO
    chunks = width // LANES
    land_dev = land_rows // n
    per_chunk = LANES // (width // n)
    per_owner = slot_reach.shape[0] * LANES // n
    twins = LANES // per_owner
    reach_rows = reach_v.shape[0]

    barrier = pltpu.get_barrier_semaphore()
    for k in range(1, n):
        pl.semaphore_signal(
            barrier, inc=1, device_id={"tile": lax.rem(me + k, n)}, device_id_type=MESH
        )

    land_copies = [
        pltpu.make_async_copy(ref, land_in.at[i], land_sem.at[i])
        for i, ref in enumerate((precip, pet, soil_init, ksat))
    ]
    land_copies.append(pltpu.make_async_copy(land_mask, mask_in, land_sem.at[4]))
    for copy in land_copies:
        copy.start()
    fields = ((head_init, h), (subsurface_init, s), (conduct, g), (drain_rate, d), (flow_code, code))
    own = [
        pltpu.make_async_copy(src, dst.at[pl.ds(HALO, rows)], own_sem.at[i])
        for i, (src, dst) in enumerate(fields)
    ]
    own.append(pltpu.make_async_copy(channel_share, share_v, own_sem.at[5]))
    own.append(pltpu.make_async_copy(cell_slot, slot_v, own_sem.at[6]))
    own.append(pltpu.make_async_copy(slot_reach.at[me // twins], places.at[me], own_sem.at[7]))
    for copy in own:
        copy.start()

    @pl.when(me == 0)
    def _():
        for _, dst in fields:
            dst[:HALO, :] = jnp.zeros((HALO, width), dst.dtype)

    @pl.when(me == n - 1)
    def _():
        for _, dst in fields:
            dst[full - HALO :, :] = jnp.zeros((HALO, width), dst.dtype)

    for copy in land_copies:
        copy.wait()
    rain, demand, water, conductivity = land_in[0], land_in[1], land_in[2], land_in[3]
    mask = mask_in[...].astype(jnp.float32)
    wet = 2.0 * water
    cap = conductivity * (1.0 - wet)
    runoff = mask * rain * rain / (rain + cap)
    drainage = 0.25 * mask * conductivity * (wet * wet) * (wet * wet)
    evap = mask * demand * wet
    soil_v[...] = water + 0.1 * (mask * rain - runoff - drainage - evap)
    soil_copy = pltpu.make_async_copy(soil_v, soil_out, out_sem.at[0])
    soil_copy.start()
    lane = lax.broadcasted_iota(jnp.int32, (cols, land_rows), 1)
    place = lax.rem(lane, land_dev)
    side = HALO // 4
    if 4 * cols < LANES:
        pack[4 * cols :, :] = jnp.zeros((LANES - 4 * cols, land_rows), jnp.float32)
    for i, x in enumerate((runoff, drainage)):
        pack[i * cols : (i + 1) * cols, :] = x
        before = jnp.where(lane >= land_dev, pltpu.roll(x, side, 1), 0.0)
        after = jnp.where(
            lane < land_rows - land_dev, pltpu.roll(x, land_rows - (land_dev - side), 1), 0.0
        )
        pack[(2 + i) * cols : (3 + i) * cols, :] = jnp.where(place < side, before, after)
    land_send[...] = jnp.transpose(pack[...]).reshape(n, land_dev, LANES)

    pl.semaphore_wait(barrier, n - 1)
    sent = []
    for k in range(1, n):
        peer = lax.rem(me + k, n)
        copy = pltpu.make_async_remote_copy(
            src_ref=land_send.at[peer],
            dst_ref=land_recv.at[lax.rem(me, per_chunk), me // per_chunk],
            send_sem=a2a_send.at[0, k],
            recv_sem=a2a_recv.at[0, k],
            device_id={"tile": peer},
            device_id_type=MESH,
        )
        copy.start()
        sent.append(copy)

    def halo_copy(i, up):
        src, dst = fields[i]
        if up:
            start, land, peer = (rows - HALO, 0, me + 1)
        else:
            start, land, peer = (0, full - HALO, me - 1)
        return pltpu.make_async_remote_copy(
            src_ref=src.at[pl.ds(start, HALO)],
            dst_ref=dst.at[pl.ds(land, HALO)],
            send_sem=halo_send.at[0 if up else 1, i],
            recv_sem=halo_recv.at[0 if up else 1, i],
            device_id={"tile": lax.rem(peer + n, n)},
            device_id_type=MESH,
        )

    @pl.when(me < n - 1)
    def _():
        for i in range(len(fields)):
            halo_copy(i, True).start()

    @pl.when(me > 0)
    def _():
        for i in range(len(fields)):
            halo_copy(i, False).start()

    for k in range(1, n):
        peer = lax.rem(me + k, n)
        copy = pltpu.make_async_remote_copy(
            src_ref=slot_reach.at[peer // twins],
            dst_ref=places.at[me],
            send_sem=a2a_send.at[1, k],
            recv_sem=a2a_recv.at[1, k],
            device_id={"tile": peer},
            device_id_type=MESH,
        )
        copy.start()
        sent.append(copy)

    land_recv[lax.rem(me, per_chunk), me // per_chunk] = land_send[me]
    for copy in sent[: n - 1]:
        copy.wait()

    l_iota = lax.broadcasted_iota(jnp.int32, (LANES, 4 * LANES), 0)
    f_iota = lax.broadcasted_iota(jnp.int32, (LANES, 4 * LANES), 1)
    cell = lax.rem(f_iota, LANES) // 4
    group = f_iota // LANES
    total = None
    for k in range(per_chunk):
        inside = (cell >= k * cols) & (cell < (k + 1) * cols)
        spread = inside & (l_iota == group * cols + cell - k * cols)
        spread = jnp.where(spread, 1.0, 0.0).astype(jnp.bfloat16)
        block = land_recv[k].reshape(chunks * land_dev, LANES)
        for part in parts_of(block, 3):
            term = jnp.dot(part, spread, preferred_element_type=jnp.float32)
            total = term if total is None else total + term
    wide[...] = total

    for copy in own:
        copy.wait()

    @pl.when(me > 0)
    def _():
        for i in range(len(fields)):
            halo_copy(i, True).wait_recv()

    @pl.when(me < n - 1)
    def _():
        for i in range(len(fields)):
            halo_copy(i, False).wait_recv()

    row8 = lax.broadcasted_iota(jnp.int32, (8, LANES), 0)
    first = lax.broadcasted_iota(jnp.int32, (full, LANES), 1) == 0
    last = lax.broadcasted_iota(jnp.int32, (full, LANES), 1) == LANES - 1
    zero = jnp.zeros((full, LANES), jnp.float32)

    def at(c):
        return pl.ds(c * LANES, LANES)

    def above(x):
        return pltpu.roll(x, 1, 0)

    def below(x):
        return pltpu.roll(x, full - 1, 0)

    def rolled(x):
        return (pltpu.roll(x, 1, 1), pltpu.roll(x, LANES - 1, 1))

    def covering(c, i):
        base = c * land_dev
        picks = [((2 + i) * LANES, r) for r in range(side)]
        picks += [(i * LANES, r) for r in range(land_dev)]
        picks += [((2 + i) * LANES, side + r) for r in range(side)]
        groups = []
        for m in range(full // 8):
            pair = []
            for lanes, r in picks[2 * m : 2 * m + 2]:
                one = wide[base + r : base + r + 1, lanes : lanes + LANES]
                pair.append(jnp.broadcast_to(one, (8, LANES)))
            groups.append(jnp.where(row8 < 4, pair[0], pair[1]))
        return jnp.concatenate(groups, axis=0)

    def load_static(c):
        gc = g[:, at(c)]
        dc = d[:, at(c)]
        kc = code[:, at(c)]
        right = jnp.where(kc == 2, dc, 0.0)
        left = jnp.where(kc == 3, dc, 0.0)
        down = jnp.where(kc == 0, dc, 0.0)
        up = jnp.where(kc == 1, dc, 0.0)
        g_r, g_l = rolled(gc)
        return gc, down, up, right, left, g_r, g_l, pltpu.roll(right, 1, 1), pltpu.roll(left, LANES - 1, 1)

    previous = None
    current = load_static(0)
    for c in range(chunks):
        following = load_static(c + 1) if c + 1 < chunks else None
        gc, down, up, right, left, g_r, g_l, r_r, l_l = current
        g_left = jnp.where(first, zero if previous is None else previous[5], g_r)
        g_right = jnp.where(last, zero if following is None else following[6], g_l)
        around = above(gc) + below(gc) + g_left + g_right
        keep_h[:, at(c)] = 1.0 - gc * around
        keep_s[:, at(c)] = 1.0 - (down + up + right + left)
        from_up[:, at(c)] = above(down)
        from_down[:, at(c)] = below(up)
        from_left[:, at(c)] = jnp.where(first, zero if previous is None else previous[7], r_r)
        from_right[:, at(c)] = jnp.where(last, zero if following is None else following[8], l_l)
        h[:, at(c)] = h[:, at(c)] + covering(c, 0)
        s[:, at(c)] = s[:, at(c)] + covering(c, 1)
        previous, current = current, following

    def load_state(c):
        hc = h[:, at(c)]
        sc = s[:, at(c)]
        gc = g[:, at(c)]
        pc = gc * hc
        return (hc, sc, gc, pc) + rolled(pc) + rolled(sc)

    def substep(_, carry):
        previous = None
        current = load_state(0)
        for c in range(chunks):
            following = load_state(c + 1) if c + 1 < chunks else None
            hc, sc, gc, pc, p_r, p_l, s_r, s_l = current
            p_left = jnp.where(first, zero if previous is None else previous[4], p_r)
            p_right = jnp.where(last, zero if following is None else following[5], p_l)
            s_left = jnp.where(first, zero if previous is None else previous[6], s_r)
            s_right = jnp.where(last, zero if following is None else following[7], s_l)
            flux = (above(pc) + below(pc)) + (p_left + p_right)
            h[:, at(c)] = keep_h[:, at(c)] * hc + gc * flux
            moved = from_up[:, at(c)] * above(sc) + from_down[:, at(c)] * below(sc)
            moved = moved + from_left[:, at(c)] * s_left + from_right[:, at(c)] * s_right
            s[:, at(c)] = keep_s[:, at(c)] * sc + moved
            previous, current = current, following
        return carry

    lax.fori_loop(0, ITERS, substep, 0)

    sub_copy = pltpu.make_async_copy(s.at[pl.ds(HALO, rows)], sub_out, out_sem.at[1])
    sub_copy.start()
    water_now = h[HALO : HALO + rows, :]
    taken = share_v[...] * water_now
    inflow[...] = taken
    head_v[...] = water_now - taken
    head_copy = pltpu.make_async_copy(head_v, head_out, out_sem.at[2])
    head_copy.start()

    owner_line = lax.broadcasted_iota(jnp.int32, (n, width), 0)
    place_line = lax.broadcasted_iota(jnp.int32, (per_owner, width), 0)

    def add_row(r, total):
        value = inflow[pl.ds(r, 1), :]
        slot = slot_v[pl.ds(r, 1), :]
        owner = slot // per_owner
        spot = slot - owner * per_owner
        left = jnp.where(owner_line == owner, value, 0.0)
        left = jnp.concatenate(parts_of(left, 2), axis=0)
        right = jnp.where(place_line == spot, 1.0, 0.0).astype(jnp.bfloat16)
        return total + lax.dot_general(left, right, NT, preferred_element_type=jnp.float32)

    total = lax.fori_loop(0, rows, add_row, jnp.zeros((2 * n, per_owner), jnp.float32))
    sums = total[:n] + total[n:]
    sums = jnp.concatenate([sums] * twins, axis=1)
    for k in range(n):
        sums_send[k] = sums[k : k + 1, :]
    sums_recv[me] = sums_send[me]
    last_sent = []
    for k in range(1, n):
        peer = lax.rem(me + k, n)
        copy = pltpu.make_async_remote_copy(
            src_ref=sums_send.at[peer],
            dst_ref=sums_recv.at[me],
            send_sem=a2a_send.at[2, k],
            recv_sem=a2a_recv.at[2, k],
            device_id={"tile": peer},
            device_id_type=MESH,
        )
        copy.start()
        last_sent.append(copy)

    for copy in sent[n - 1 :]:
        copy.wait()
    half = lax.broadcasted_iota(jnp.int32, (1, LANES), 1) // per_owner == lax.rem(me, twins)
    lane_line = lax.broadcasted_iota(jnp.int32, (LANES, LANES), 0)
    reach_line = lax.broadcasted_iota(jnp.int32, (reach_rows, LANES), 0)
    for j in range(n):
        there = places[j]
        low = lax.rem(there, LANES)
        spots[:, at(j)] = jnp.where(half & (lane_line == low), 1.0, 0.0).astype(jnp.bfloat16)
    for copy in last_sent:
        copy.wait()
    found = []
    for j in range(n):
        high = places[j] // LANES
        found.append(jnp.where(reach_line == high, sums_recv[j], 0.0))
    found = jnp.concatenate(parts_of(jnp.concatenate(found, axis=1), 3), axis=0)
    reach = lax.dot_general(found, spots[...], NT, preferred_element_type=jnp.float32)
    reach_v[...] = reach[:reach_rows] + reach[reach_rows : 2 * reach_rows] + reach[2 * reach_rows :]
    reach_copy = pltpu.make_async_copy(reach_v, reach_out, out_sem.at[3])
    reach_copy.start()

    @pl.when(me < n - 1)
    def _():
        for i in range(len(fields)):
            halo_copy(i, True).wait_send()

    @pl.when(me > 0)
    def _():
        for i in range(len(fields)):
            halo_copy(i, False).wait_send()

    for copy in (soil_copy, sub_copy, head_copy, reach_copy):
        copy.wait()


def local(*args):
    n = lax.axis_size("tile")
    precip, head_init, slot_reach = args[0], args[5], args[12]
    cols, land_rows = precip.shape
    rows, width = head_init.shape
    slots = slot_reach.shape[0]
    full = rows + 2 * HALO
    land_dev = land_rows // n
    per_chunk = LANES // (width // n)
    chunks = width // LANES
    f32, i32 = jnp.float32, jnp.int32
    tall = pltpu.VMEM((full, width), f32)
    own = pltpu.VMEM((rows, width), f32)
    anywhere = pl.BlockSpec(memory_space=pl.ANY)
    soil, head, sub, reach = pl.pallas_call(
        functools.partial(kernel, n),
        out_shape=(
            jax.ShapeDtypeStruct(precip.shape, f32),
            jax.ShapeDtypeStruct(head_init.shape, f32),
            jax.ShapeDtypeStruct(head_init.shape, f32),
            jax.ShapeDtypeStruct((slots // LANES, LANES), f32),
        ),
        in_specs=[anywhere] * 13,
        out_specs=(anywhere,) * 4,
        scratch_shapes=[
            pltpu.VMEM((4, cols, land_rows), f32),
            pltpu.VMEM((cols, land_rows), i32),
            pltpu.VMEM((cols, land_rows), f32),
            pltpu.VMEM((LANES, land_rows), f32),
            pltpu.VMEM((n, land_dev, LANES), f32),
            pltpu.VMEM((per_chunk, chunks, land_dev, LANES), f32),
            pltpu.VMEM((chunks * land_dev, 4 * LANES), f32),
            tall,
            tall,
            tall,
            tall,
            pltpu.VMEM((full, width), i32),
            tall,
            tall,
            tall,
            tall,
            tall,
            tall,
            own,
            pltpu.VMEM((rows, width), i32),
            own,
            own,
            pltpu.VMEM((n, 1, LANES), f32),
            pltpu.VMEM((n, 1, LANES), f32),
            pltpu.VMEM((n, 1, LANES), i32),
            pltpu.VMEM((LANES, n * LANES), jnp.bfloat16),
            pltpu.VMEM((slots // LANES, LANES), f32),
            pltpu.SemaphoreType.DMA((5,)),
            pltpu.SemaphoreType.DMA((8,)),
            pltpu.SemaphoreType.DMA((2, 5)),
            pltpu.SemaphoreType.DMA((2, 5)),
            pltpu.SemaphoreType.DMA((3, n)),
            pltpu.SemaphoreType.DMA((3, n)),
            pltpu.SemaphoreType.DMA((4,)),
        ],
        compiler_params=pltpu.CompilerParams(collective_id=0, has_side_effects=True),
        name="step",
    )(*args[:12], slot_reach.reshape(slots // LANES, 1, LANES))
    return soil, head, sub, reach.reshape(slots)


def solution(mesh):
    grid = P(("member", "tile"), None)
    line = P(("member", "tile"))
    return jax.shard_map(
        local,
        mesh=mesh,
        in_specs=(grid,) * 12 + (line,),
        out_specs=(grid, grid, grid, line),
        check_vma=False,
    )
```

```python
import functools

import jax
import jax.numpy as jnp
from jax import lax
from jax.experimental import pallas as pl
from jax.experimental.pallas import tpu as pltpu
from jax.sharding import PartitionSpec as P

ITERS = 6
HALO = 8
LANES = 128
MESH = pl.DeviceIdType.MESH
NT = (((1,), (1,)), ((), ()))


def parts_of(x, count):
    parts = []
    for _ in range(count):
        part = x.astype(jnp.bfloat16)
        parts.append(part)
        x = x - part.astype(jnp.float32)
    return parts


def kernel(
    n,
    precip,
    pet,
    soil_init,
    ksat,
    land_mask,
    head_init,
    subsurface_init,
    conduct,
    drain_rate,
    flow_code,
    channel_share,
    cell_slot,
    slot_reach,
    soil_out,
    head_out,
    sub_out,
    reach_out,
    land_in,
    mask_in,
    pack,
    land_send,
    land_recv,
    wide,
    h,
    s,
    g,
    d,
    code,
    keep_h,
    keep_s,
    from_up,
    from_down,
    from_left,
    from_right,
    share_v,
    slot_v,
    inflow,
    sums_send,
    sums_recv,
    places,
    spots,
    land_sem,
    own_sem,
    halo_send,
    halo_recv,
    a2a_send,
    a2a_recv,
):
    me = lax.axis_index("tile")
    cols, land_rows = precip.shape
    rows, width = head_init.shape
    full = rows + 2 * HALO
    chunks = width // LANES
    land_dev = land_rows // n
    per_chunk = LANES // (width // n)
    per_owner = slot_reach.shape[0] * LANES // n
    twins = LANES // per_owner
    reach_rows = reach_out.shape[0]

    barrier = pltpu.get_barrier_semaphore()
    for k in range(1, n):
        pl.semaphore_signal(
            barrier, inc=1, device_id={"tile": lax.rem(me + k, n)}, device_id_type=MESH
        )

    land_copies = [
        pltpu.make_async_copy(ref, land_in.at[i], land_sem.at[i])
        for i, ref in enumerate((precip, pet, soil_init, ksat))
    ]
    land_copies.append(pltpu.make_async_copy(land_mask, mask_in, land_sem.at[4]))
    for copy in land_copies:
        copy.start()
    fields = ((head_init, h), (subsurface_init, s), (conduct, g), (drain_rate, d), (flow_code, code))
    own = [
        pltpu.make_async_copy(src, dst.at[pl.ds(HALO, rows)], own_sem.at[i])
        for i, (src, dst) in enumerate(fields)
    ]
    own.append(pltpu.make_async_copy(channel_share, share_v, own_sem.at[5]))
    own.append(pltpu.make_async_copy(cell_slot, slot_v, own_sem.at[6]))
    own.append(pltpu.make_async_copy(slot_reach.at[me // twins], places.at[me], own_sem.at[7]))
    for copy in own:
        copy.start()

    @pl.when(me == 0)
    def _():
        for _, dst in fields:
            dst[:HALO, :] = jnp.zeros((HALO, width), dst.dtype)

    @pl.when(me == n - 1)
    def _():
        for _, dst in fields:
            dst[full - HALO :, :] = jnp.zeros((HALO, width), dst.dtype)

    for copy in land_copies:
        copy.wait()
    rain, demand, water, conductivity = land_in[0], land_in[1], land_in[2], land_in[3]
    mask = mask_in[...].astype(jnp.float32)
    wet = 2.0 * water
    cap = conductivity * (1.0 - wet)
    runoff = mask * rain * rain / (rain + cap)
    drainage = 0.25 * mask * conductivity * (wet * wet) * (wet * wet)
    evap = mask * demand * wet
    soil_out[...] = water + 0.1 * (mask * rain - runoff - drainage - evap)
    lane = lax.broadcasted_iota(jnp.int32, (cols, land_rows), 1)
    place = lax.rem(lane, land_dev)
    side = HALO // 4
    if 4 * cols < LANES:
        pack[4 * cols :, :] = jnp.zeros((LANES - 4 * cols, land_rows), jnp.float32)
    for i, x in enumerate((runoff, drainage)):
        pack[i * cols : (i + 1) * cols, :] = x
        before = jnp.where(lane >= land_dev, pltpu.roll(x, side, 1), 0.0)
        after = jnp.where(
            lane < land_rows - land_dev, pltpu.roll(x, land_rows - (land_dev - side), 1), 0.0
        )
        pack[(2 + i) * cols : (3 + i) * cols, :] = jnp.where(place < side, before, after)
    land_send[...] = jnp.transpose(pack[...]).reshape(n, land_dev, LANES)

    pl.semaphore_wait(barrier, n - 1)
    sent = []
    for k in range(1, n):
        peer = lax.rem(me + k, n)
        copy = pltpu.make_async_remote_copy(
            src_ref=land_send.at[peer],
            dst_ref=land_recv.at[lax.rem(me, per_chunk), me // per_chunk],
            send_sem=a2a_send.at[0, k],
            recv_sem=a2a_recv.at[0, k],
            device_id={"tile": peer},
            device_id_type=MESH,
        )
        copy.start()
        sent.append(copy)

    def halo_copy(i, up):
        src, dst = fields[i]
        if up:
            start, land, peer = (rows - ITERS, HALO - ITERS, me + 1)
        else:
            start, land, peer = (0, full - HALO, me - 1)
        return pltpu.make_async_remote_copy(
            src_ref=src.at[pl.ds(start, ITERS)],
            dst_ref=dst.at[pl.ds(land, ITERS)],
            send_sem=halo_send.at[0 if up else 1, i],
            recv_sem=halo_recv.at[0 if up else 1, i],
            device_id={"tile": lax.rem(peer + n, n)},
            device_id_type=MESH,
        )

    @pl.when(me < n - 1)
    def _():
        for i in range(len(fields)):
            halo_copy(i, True).start()

    @pl.when(me > 0)
    def _():
        for i in range(len(fields)):
            halo_copy(i, False).start()

    for k in range(1, n):
        peer = lax.rem(me + k, n)
        copy = pltpu.make_async_remote_copy(
            src_ref=slot_reach.at[peer // twins],
            dst_ref=places.at[me],
            send_sem=a2a_send.at[1, k],
            recv_sem=a2a_recv.at[1, k],
            device_id={"tile": peer},
            device_id_type=MESH,
        )
        copy.start()
        sent.append(copy)

    land_recv[lax.rem(me, per_chunk), me // per_chunk] = land_send[me]
    for copy in sent[: n - 1]:
        copy.wait()

    l_iota = lax.broadcasted_iota(jnp.int32, (LANES, 4 * LANES), 0)
    f_iota = lax.broadcasted_iota(jnp.int32, (LANES, 4 * LANES), 1)
    cell = lax.rem(f_iota, LANES) // 4
    group = f_iota // LANES
    total = None
    for k in range(per_chunk):
        inside = (cell >= k * cols) & (cell < (k + 1) * cols)
        spread = inside & (l_iota == group * cols + cell - k * cols)
        spread = jnp.where(spread, 1.0, 0.0).astype(jnp.bfloat16)
        block = land_recv[k].reshape(chunks * land_dev, LANES)
        for part in parts_of(block, 3):
            term = jnp.dot(part, spread, preferred_element_type=jnp.float32)
            total = term if total is None else total + term
    wide[...] = total

    for copy in own:
        copy.wait()

    @pl.when(me > 0)
    def _():
        for i in range(len(fields)):
            halo_copy(i, True).wait_recv()

    @pl.when(me < n - 1)
    def _():
        for i in range(len(fields)):
            halo_copy(i, False).wait_recv()

    row8 = lax.broadcasted_iota(jnp.int32, (8, LANES), 0)
    first = lax.broadcasted_iota(jnp.int32, (full, LANES), 1) == 0
    last = lax.broadcasted_iota(jnp.int32, (full, LANES), 1) == LANES - 1
    zero = jnp.zeros((full, LANES), jnp.float32)

    def at(c):
        return pl.ds(c * LANES, LANES)

    def above(x):
        return pltpu.roll(x, 1, 0)

    def below(x):
        return pltpu.roll(x, full - 1, 0)

    def rolled(x):
        return (pltpu.roll(x, 1, 1), pltpu.roll(x, LANES - 1, 1))

    def covering(c, i):
        base = c * land_dev
        picks = [((2 + i) * LANES, r) for r in range(side)]
        picks += [(i * LANES, r) for r in range(land_dev)]
        picks += [((2 + i) * LANES, side + r) for r in range(side)]
        groups = []
        for m in range(full // 8):
            pair = []
            for lanes, r in picks[2 * m : 2 * m + 2]:
                one = wide[base + r : base + r + 1, lanes : lanes + LANES]
                pair.append(jnp.broadcast_to(one, (8, LANES)))
            groups.append(jnp.where(row8 < 4, pair[0], pair[1]))
        return jnp.concatenate(groups, axis=0)

    def load_static(c):
        gc = g[:, at(c)]
        dc = d[:, at(c)]
        kc = code[:, at(c)]
        right = jnp.where(kc == 2, dc, 0.0)
        left = jnp.where(kc == 3, dc, 0.0)
        down = jnp.where(kc == 0, dc, 0.0)
        up = jnp.where(kc == 1, dc, 0.0)
        g_r, g_l = rolled(gc)
        return gc, down, up, right, left, g_r, g_l, pltpu.roll(right, 1, 1), pltpu.roll(left, LANES - 1, 1)

    previous = None
    current = load_static(0)
    for c in range(chunks):
        following = load_static(c + 1) if c + 1 < chunks else None
        gc, down, up, right, left, g_r, g_l, r_r, l_l = current
        g_left = jnp.where(first, zero if previous is None else previous[5], g_r)
        g_right = jnp.where(last, zero if following is None else following[6], g_l)
        around = above(gc) + below(gc) + g_left + g_right
        keep_h[:, at(c)] = 1.0 - gc * around
        keep_s[:, at(c)] = 1.0 - (down + up + right + left)
        from_up[:, at(c)] = above(down)
        from_down[:, at(c)] = below(up)
        from_left[:, at(c)] = jnp.where(first, zero if previous is None else previous[7], r_r)
        from_right[:, at(c)] = jnp.where(last, zero if following is None else following[8], l_l)
        h[:, at(c)] = h[:, at(c)] + covering(c, 0)
        s[:, at(c)] = s[:, at(c)] + covering(c, 1)
        previous, current = current, following

    def load_state(c):
        hc = h[:, at(c)]
        sc = s[:, at(c)]
        gc = g[:, at(c)]
        pc = gc * hc
        return (hc, sc, gc, pc) + rolled(pc) + rolled(sc)

    def substep(_, carry):
        previous = None
        current = load_state(0)
        for c in range(chunks):
            following = load_state(c + 1) if c + 1 < chunks else None
            hc, sc, gc, pc, p_r, p_l, s_r, s_l = current
            p_left = jnp.where(first, zero if previous is None else previous[4], p_r)
            p_right = jnp.where(last, zero if following is None else following[5], p_l)
            s_left = jnp.where(first, zero if previous is None else previous[6], s_r)
            s_right = jnp.where(last, zero if following is None else following[7], s_l)
            flux = (above(pc) + below(pc)) + (p_left + p_right)
            h[:, at(c)] = keep_h[:, at(c)] * hc + gc * flux
            moved = from_up[:, at(c)] * above(sc) + from_down[:, at(c)] * below(sc)
            moved = moved + from_left[:, at(c)] * s_left + from_right[:, at(c)] * s_right
            s[:, at(c)] = keep_s[:, at(c)] * sc + moved
            previous, current = current, following
        return carry

    lax.fori_loop(0, ITERS, substep, 0)

    sub_out[...] = s[HALO : HALO + rows, :]
    water_now = h[HALO : HALO + rows, :]
    taken = share_v[...] * water_now
    inflow[...] = taken
    head_out[...] = water_now - taken

    owner_line = lax.broadcasted_iota(jnp.int32, (n, width), 0)
    place_line = lax.broadcasted_iota(jnp.int32, (per_owner, width), 0)

    def add_row(r, total):
        value = inflow[pl.ds(r, 1), :]
        slot = slot_v[pl.ds(r, 1), :]
        owner = slot // per_owner
        spot = slot - owner * per_owner
        left = jnp.where(owner_line == owner, value, 0.0)
        left = jnp.concatenate(parts_of(left, 2), axis=0)
        right = jnp.where(place_line == spot, 1.0, 0.0).astype(jnp.bfloat16)
        return total + lax.dot_general(left, right, NT, preferred_element_type=jnp.float32)

    total = lax.fori_loop(0, rows, add_row, jnp.zeros((2 * n, per_owner), jnp.float32), unroll=8)
    sums = total[:n] + total[n:]
    sums = jnp.concatenate([sums] * twins, axis=1)
    for k in range(n):
        sums_send[k] = sums[k : k + 1, :]
    sums_recv[me] = sums_send[me]
    last_sent = []
    for k in range(1, n):
        peer = lax.rem(me + k, n)
        copy = pltpu.make_async_remote_copy(
            src_ref=sums_send.at[peer],
            dst_ref=sums_recv.at[me],
            send_sem=a2a_send.at[2, k],
            recv_sem=a2a_recv.at[2, k],
            device_id={"tile": peer},
            device_id_type=MESH,
        )
        copy.start()
        last_sent.append(copy)

    for copy in sent[n - 1 :]:
        copy.wait()
    half = lax.broadcasted_iota(jnp.int32, (1, LANES), 1) // per_owner == lax.rem(me, twins)
    lane_line = lax.broadcasted_iota(jnp.int32, (LANES, LANES), 0)
    reach_line = lax.broadcasted_iota(jnp.int32, (reach_rows, LANES), 0)
    for j in range(n):
        there = places[j]
        low = lax.rem(there, LANES)
        spots[:, at(j)] = jnp.where(half & (lane_line == low), 1.0, 0.0).astype(jnp.bfloat16)
    for copy in last_sent:
        copy.wait()
    found = []
    for j in range(n):
        high = places[j] // LANES
        found.append(jnp.where(reach_line == high, sums_recv[j], 0.0))
    found = jnp.concatenate(parts_of(jnp.concatenate(found, axis=1), 3), axis=0)
    reach = lax.dot_general(found, spots[...], NT, preferred_element_type=jnp.float32)
    reach_out[...] = reach[:reach_rows] + reach[reach_rows : 2 * reach_rows] + reach[2 * reach_rows :]

    @pl.when(me < n - 1)
    def _():
        for i in range(len(fields)):
            halo_copy(i, True).wait_send()

    @pl.when(me > 0)
    def _():
        for i in range(len(fields)):
            halo_copy(i, False).wait_send()


def local(*args):
    n = lax.axis_size("tile")
    precip, head_init, slot_reach = args[0], args[5], args[12]
    cols, land_rows = precip.shape
    rows, width = head_init.shape
    slots = slot_reach.shape[0]
    full = rows + 2 * HALO
    land_dev = land_rows // n
    per_chunk = LANES // (width // n)
    chunks = width // LANES
    f32, i32 = jnp.float32, jnp.int32
    tall = pltpu.VMEM((full, width), f32)
    own = pltpu.VMEM((rows, width), f32)
    anywhere = pl.BlockSpec(memory_space=pl.ANY)
    soil, head, sub, reach = pl.pallas_call(
        functools.partial(kernel, n),
        out_shape=(
            pltpu.VMEM(precip.shape, f32),
            pltpu.VMEM(head_init.shape, f32),
            pltpu.VMEM(head_init.shape, f32),
            pltpu.VMEM((slots // LANES, LANES), f32),
        ),
        in_specs=[anywhere] * 13,
        out_specs=(pl.BlockSpec(memory_space=pltpu.VMEM),) * 4,
        scratch_shapes=[
            pltpu.VMEM((4, cols, land_rows), f32),
            pltpu.VMEM((cols, land_rows), i32),
            pltpu.VMEM((LANES, land_rows), f32),
            pltpu.VMEM((n, land_dev, LANES), f32),
            pltpu.VMEM((per_chunk, chunks, land_dev, LANES), f32),
            pltpu.VMEM((chunks * land_dev, 4 * LANES), f32),
            tall,
            tall,
            tall,
            tall,
            pltpu.VMEM((full, width), i32),
            tall,
            tall,
            tall,
            tall,
            tall,
            tall,
            own,
            pltpu.VMEM((rows, width), i32),
            own,
            pltpu.VMEM((n, 1, LANES), f32),
            pltpu.VMEM((n, 1, LANES), f32),
            pltpu.VMEM((n, 1, LANES), i32),
            pltpu.VMEM((LANES, n * LANES), jnp.bfloat16),
            pltpu.SemaphoreType.DMA((5,)),
            pltpu.SemaphoreType.DMA((8,)),
            pltpu.SemaphoreType.DMA((2, 5)),
            pltpu.SemaphoreType.DMA((2, 5)),
            pltpu.SemaphoreType.DMA((3, n)),
            pltpu.SemaphoreType.DMA((3, n)),
        ],
        compiler_params=pltpu.CompilerParams(collective_id=0, has_side_effects=True, vmem_limit_bytes=16 * 2**20),
        name="step",
    )(*[pltpu.with_memory_space_constraint(x, pltpu.HBM) for x in (*args[:12], slot_reach.reshape(slots // LANES, 1, LANES))])
    return soil, head, sub, reach.reshape(slots)


def solution(mesh):
    grid = P(("member", "tile"), None)
    line = P(("member", "tile"))
    return jax.shard_map(
        local,
        mesh=mesh,
        in_specs=(grid,) * 12 + (line,),
        out_specs=(grid, grid, grid, line),
        check_vma=False,
    )
```

```python
import functools

import jax
import jax.numpy as jnp
from jax import lax
from jax.experimental import pallas as pl
from jax.experimental.pallas import tpu as pltpu
from jax.sharding import PartitionSpec as P

ITERS = 6
HALO = 8
LANES = 128
MESH = pl.DeviceIdType.MESH
NT = (((1,), (1,)), ((), ()))


def parts_of(x, count):
    parts = []
    for _ in range(count):
        part = x.astype(jnp.bfloat16)
        parts.append(part)
        x = x - part.astype(jnp.float32)
    return parts


def kernel(
    n,
    precip,
    pet,
    soil_init,
    ksat,
    land_mask,
    head_init,
    subsurface_init,
    conduct,
    drain_rate,
    flow_code,
    channel_share,
    cell_slot,
    slot_reach,
    soil_out,
    head_out,
    sub_out,
    reach_out,
    land_in,
    mask_in,
    pack,
    land_send,
    land_recv,
    wide,
    h,
    s,
    g,
    d,
    code,
    keep_h,
    keep_s,
    from_up,
    from_down,
    from_left,
    from_right,
    share_v,
    slot_v,
    high_v,
    rest_v,
    owner_v,
    spot_v,
    sums_send,
    sums_recv,
    places,
    spots,
    land_sem,
    own_sem,
    halo_send,
    halo_recv,
    a2a_send,
    a2a_recv,
):
    me = lax.axis_index("tile")
    cols, land_rows = precip.shape
    rows, width = head_init.shape
    full = rows + 2 * HALO
    chunks = width // LANES
    land_dev = land_rows // n
    per_chunk = LANES // (width // n)
    per_owner = slot_reach.shape[0] * LANES // n
    twins = LANES // per_owner
    reach_rows = reach_out.shape[0]

    barrier = pltpu.get_barrier_semaphore()
    for k in range(1, n):
        pl.semaphore_signal(
            barrier, inc=1, device_id={"tile": lax.rem(me + k, n)}, device_id_type=MESH
        )

    land_copies = [
        pltpu.make_async_copy(ref, land_in.at[i], land_sem.at[i])
        for i, ref in enumerate((precip, pet, soil_init, ksat))
    ]
    land_copies.append(pltpu.make_async_copy(land_mask, mask_in, land_sem.at[4]))
    for copy in land_copies:
        copy.start()
    fields = ((head_init, h), (subsurface_init, s), (conduct, g), (drain_rate, d), (flow_code, code))
    own = [
        pltpu.make_async_copy(src, dst.at[pl.ds(HALO, rows)], own_sem.at[i])
        for i, (src, dst) in enumerate(fields)
    ]
    own.append(pltpu.make_async_copy(channel_share, share_v, own_sem.at[5]))
    own.append(pltpu.make_async_copy(cell_slot, slot_v, own_sem.at[6]))
    own.append(pltpu.make_async_copy(slot_reach.at[me // twins], places.at[me], own_sem.at[7]))
    for copy in own:
        copy.start()

    @pl.when(me == 0)
    def _():
        for _, dst in fields:
            dst[:HALO, :] = jnp.zeros((HALO, width), dst.dtype)

    @pl.when(me == n - 1)
    def _():
        for _, dst in fields:
            dst[full - HALO :, :] = jnp.zeros((HALO, width), dst.dtype)

    for copy in land_copies:
        copy.wait()
    rain, demand, water, conductivity = land_in[0], land_in[1], land_in[2], land_in[3]
    mask = mask_in[...].astype(jnp.float32)
    wet = 2.0 * water
    cap = conductivity * (1.0 - wet)
    runoff = mask * rain * rain / (rain + cap)
    drainage = 0.25 * mask * conductivity * (wet * wet) * (wet * wet)
    evap = mask * demand * wet
    soil_out[...] = water + 0.1 * (mask * rain - runoff - drainage - evap)
    lane = lax.broadcasted_iota(jnp.int32, (cols, land_rows), 1)
    place = lax.rem(lane, land_dev)
    side = HALO // 4
    if 4 * cols < LANES:
        pack[4 * cols :, :] = jnp.zeros((LANES - 4 * cols, land_rows), jnp.float32)
    for i, x in enumerate((runoff, drainage)):
        pack[i * cols : (i + 1) * cols, :] = x
        before = jnp.where(lane >= land_dev, pltpu.roll(x, side, 1), 0.0)
        after = jnp.where(
            lane < land_rows - land_dev, pltpu.roll(x, land_rows - (land_dev - side), 1), 0.0
        )
        pack[(2 + i) * cols : (3 + i) * cols, :] = jnp.where(place < side, before, after)
    land_send[...] = jnp.transpose(pack[...]).reshape(n, land_dev, LANES)

    pl.semaphore_wait(barrier, n - 1)
    sent = []
    for k in range(1, n):
        peer = lax.rem(me + k, n)
        copy = pltpu.make_async_remote_copy(
            src_ref=land_send.at[peer],
            dst_ref=land_recv.at[lax.rem(me, per_chunk), me // per_chunk],
            send_sem=a2a_send.at[0, k],
            recv_sem=a2a_recv.at[0, k],
            device_id={"tile": peer},
            device_id_type=MESH,
        )
        copy.start()
        sent.append(copy)

    def halo_copy(i, up):
        src, dst = fields[i]
        if up:
            start, land, peer = (rows - ITERS, HALO - ITERS, me + 1)
        else:
            start, land, peer = (0, full - HALO, me - 1)
        return pltpu.make_async_remote_copy(
            src_ref=src.at[pl.ds(start, ITERS)],
            dst_ref=dst.at[pl.ds(land, ITERS)],
            send_sem=halo_send.at[0 if up else 1, i],
            recv_sem=halo_recv.at[0 if up else 1, i],
            device_id={"tile": lax.rem(peer + n, n)},
            device_id_type=MESH,
        )

    @pl.when(me < n - 1)
    def _():
        for i in range(len(fields)):
            halo_copy(i, True).start()

    @pl.when(me > 0)
    def _():
        for i in range(len(fields)):
            halo_copy(i, False).start()

    for k in range(1, n):
        peer = lax.rem(me + k, n)
        copy = pltpu.make_async_remote_copy(
            src_ref=slot_reach.at[peer // twins],
            dst_ref=places.at[me],
            send_sem=a2a_send.at[1, k],
            recv_sem=a2a_recv.at[1, k],
            device_id={"tile": peer},
            device_id_type=MESH,
        )
        copy.start()
        sent.append(copy)

    land_recv[lax.rem(me, per_chunk), me // per_chunk] = land_send[me]
    for copy in sent[: n - 1]:
        copy.wait()

    l_iota = lax.broadcasted_iota(jnp.int32, (LANES, 4 * LANES), 0)
    f_iota = lax.broadcasted_iota(jnp.int32, (LANES, 4 * LANES), 1)
    cell = lax.rem(f_iota, LANES) // 4
    group = f_iota // LANES
    total = None
    for k in range(per_chunk):
        inside = (cell >= k * cols) & (cell < (k + 1) * cols)
        spread = inside & (l_iota == group * cols + cell - k * cols)
        spread = jnp.where(spread, 1.0, 0.0).astype(jnp.bfloat16)
        block = land_recv[k].reshape(chunks * land_dev, LANES)
        for part in parts_of(block, 3):
            term = jnp.dot(part, spread, preferred_element_type=jnp.float32)
            total = term if total is None else total + term
    wide[...] = total

    for copy in own:
        copy.wait()
    slot = slot_v[...]
    owner = slot // per_owner
    owner_v[...] = owner.astype(jnp.float32)
    spot_v[...] = (slot - owner * per_owner).astype(jnp.float32)

    @pl.when(me > 0)
    def _():
        for i in range(len(fields)):
            halo_copy(i, True).wait_recv()

    @pl.when(me < n - 1)
    def _():
        for i in range(len(fields)):
            halo_copy(i, False).wait_recv()

    row8 = lax.broadcasted_iota(jnp.int32, (8, LANES), 0)
    first = lax.broadcasted_iota(jnp.int32, (full, LANES), 1) == 0
    last = lax.broadcasted_iota(jnp.int32, (full, LANES), 1) == LANES - 1
    zero = jnp.zeros((full, LANES), jnp.float32)

    def at(c):
        return pl.ds(c * LANES, LANES)

    def above(x):
        return pltpu.roll(x, 1, 0)

    def below(x):
        return pltpu.roll(x, full - 1, 0)

    def rolled(x):
        return (pltpu.roll(x, 1, 1), pltpu.roll(x, LANES - 1, 1))

    def covering(c, i):
        base = c * land_dev
        picks = [((2 + i) * LANES, r) for r in range(side)]
        picks += [(i * LANES, r) for r in range(land_dev)]
        picks += [((2 + i) * LANES, side + r) for r in range(side)]
        groups = []
        for m in range(full // 8):
            pair = []
            for lanes, r in picks[2 * m : 2 * m + 2]:
                one = wide[base + r : base + r + 1, lanes : lanes + LANES]
                pair.append(jnp.broadcast_to(one, (8, LANES)))
            groups.append(jnp.where(row8 < 4, pair[0], pair[1]))
        return jnp.concatenate(groups, axis=0)

    def load_static(c):
        gc = g[:, at(c)]
        dc = d[:, at(c)]
        kc = code[:, at(c)]
        right = jnp.where(kc == 2, dc, 0.0)
        left = jnp.where(kc == 3, dc, 0.0)
        down = jnp.where(kc == 0, dc, 0.0)
        up = jnp.where(kc == 1, dc, 0.0)
        g_r, g_l = rolled(gc)
        return gc, down, up, right, left, g_r, g_l, pltpu.roll(right, 1, 1), pltpu.roll(left, LANES - 1, 1)

    previous = None
    current = load_static(0)
    for c in range(chunks):
        following = load_static(c + 1) if c + 1 < chunks else None
        gc, down, up, right, left, g_r, g_l, r_r, l_l = current
        g_left = jnp.where(first, zero if previous is None else previous[5], g_r)
        g_right = jnp.where(last, zero if following is None else following[6], g_l)
        around = above(gc) + below(gc) + g_left + g_right
        keep_h[:, at(c)] = 1.0 - gc * around
        keep_s[:, at(c)] = 1.0 - (down + up + right + left)
        from_up[:, at(c)] = above(down)
        from_down[:, at(c)] = below(up)
        from_left[:, at(c)] = jnp.where(first, zero if previous is None else previous[7], r_r)
        from_right[:, at(c)] = jnp.where(last, zero if following is None else following[8], l_l)
        h[:, at(c)] = h[:, at(c)] + covering(c, 0)
        s[:, at(c)] = s[:, at(c)] + covering(c, 1)
        previous, current = current, following

    def load_state(c):
        hc = h[:, at(c)]
        sc = s[:, at(c)]
        gc = g[:, at(c)]
        pc = gc * hc
        return (hc, sc, gc, pc) + rolled(pc) + rolled(sc)

    def substep(_, carry):
        previous = None
        current = load_state(0)
        for c in range(chunks):
            following = load_state(c + 1) if c + 1 < chunks else None
            hc, sc, gc, pc, p_r, p_l, s_r, s_l = current
            p_left = jnp.where(first, zero if previous is None else previous[4], p_r)
            p_right = jnp.where(last, zero if following is None else following[5], p_l)
            s_left = jnp.where(first, zero if previous is None else previous[6], s_r)
            s_right = jnp.where(last, zero if following is None else following[7], s_l)
            flux = (above(pc) + below(pc)) + (p_left + p_right)
            h[:, at(c)] = keep_h[:, at(c)] * hc + gc * flux
            moved = from_up[:, at(c)] * above(sc) + from_down[:, at(c)] * below(sc)
            moved = moved + from_left[:, at(c)] * s_left + from_right[:, at(c)] * s_right
            s[:, at(c)] = keep_s[:, at(c)] * sc + moved
            previous, current = current, following
        return carry

    lax.fori_loop(0, ITERS, substep, 0)

    sub_out[...] = s[HALO : HALO + rows, :]
    water_now = h[HALO : HALO + rows, :]
    taken = share_v[...] * water_now
    head_out[...] = water_now - taken

    line = lax.broadcasted_iota(jnp.int32, (16, width), 0).astype(jnp.float32)
    owner_lines = [(line + 16 * q).astype(jnp.bfloat16) for q in range(n // 16)]
    spot_lines = [(line + 16 * q).astype(jnp.bfloat16) for q in range(per_owner // 16)]
    high_v[...] = taken.astype(jnp.bfloat16).astype(jnp.float32)
    rest_v[...] = taken - high_v[...]
    one, none = jnp.ones((16, width), jnp.bfloat16), jnp.zeros((16, width), jnp.bfloat16)

    def row_of(ref, r):
        return jnp.broadcast_to(ref[pl.ds(r, 1), :], (16, width)).astype(jnp.bfloat16)

    def add_row(r, total):
        owner, spot = row_of(owner_v, r), row_of(spot_v, r)
        values = (row_of(high_v, r), row_of(rest_v, r))
        hits = [owner == x for x in owner_lines]
        left = jnp.concatenate([jnp.where(hit, x, none) for x in values for hit in hits], axis=0)
        right = jnp.concatenate([jnp.where(spot == x, one, none) for x in spot_lines], axis=0)
        return total + lax.dot_general(left, right, NT, preferred_element_type=jnp.float32)

    total = lax.fori_loop(0, rows, add_row, jnp.zeros((2 * n, per_owner), jnp.float32), unroll=8)
    sums = total[:n] + total[n:]
    sums = jnp.concatenate([sums] * twins, axis=1)
    for k in range(n):
        sums_send[k] = sums[k : k + 1, :]
    sums_recv[me] = sums_send[me]
    last_sent = []
    for k in range(1, n):
        peer = lax.rem(me + k, n)
        copy = pltpu.make_async_remote_copy(
            src_ref=sums_send.at[peer],
            dst_ref=sums_recv.at[me],
            send_sem=a2a_send.at[2, k],
            recv_sem=a2a_recv.at[2, k],
            device_id={"tile": peer},
            device_id_type=MESH,
        )
        copy.start()
        last_sent.append(copy)

    for copy in sent[n - 1 :]:
        copy.wait()
    half = lax.broadcasted_iota(jnp.int32, (1, LANES), 1) // per_owner == lax.rem(me, twins)
    lane_line = lax.broadcasted_iota(jnp.int32, (LANES, LANES), 0)
    reach_line = lax.broadcasted_iota(jnp.int32, (reach_rows, LANES), 0)
    for j in range(n):
        there = places[j]
        low = lax.rem(there, LANES)
        spots[:, at(j)] = jnp.where(half & (lane_line == low), 1.0, 0.0).astype(jnp.bfloat16)
    for copy in last_sent:
        copy.wait()
    found = []
    for j in range(n):
        high = places[j] // LANES
        found.append(jnp.where(reach_line == high, sums_recv[j], 0.0))
    found = jnp.concatenate(parts_of(jnp.concatenate(found, axis=1), 3), axis=0)
    reach = lax.dot_general(found, spots[...], NT, preferred_element_type=jnp.float32)
    reach_out[...] = reach[:reach_rows] + reach[reach_rows : 2 * reach_rows] + reach[2 * reach_rows :]

    @pl.when(me < n - 1)
    def _():
        for i in range(len(fields)):
            halo_copy(i, True).wait_send()

    @pl.when(me > 0)
    def _():
        for i in range(len(fields)):
            halo_copy(i, False).wait_send()


def flush(*refs):
    count = (len(refs) - 1) // 2
    copies = [
        pltpu.make_async_copy(src, dst, refs[-1].at[i])
        for i, (src, dst) in enumerate(zip(refs[:count], refs[count:-1]))
    ]
    for copy in copies:
        copy.start()
    for copy in copies:
        copy.wait()


def local(*args):
    n = lax.axis_size("tile")
    precip, head_init, slot_reach = args[0], args[5], args[12]
    cols, land_rows = precip.shape
    rows, width = head_init.shape
    slots = slot_reach.shape[0]
    full = rows + 2 * HALO
    land_dev = land_rows // n
    per_chunk = LANES // (width // n)
    chunks = width // LANES
    f32, i32 = jnp.float32, jnp.int32
    tall = pltpu.VMEM((full, width), f32)
    own = pltpu.VMEM((rows, width), f32)
    anywhere = pl.BlockSpec(memory_space=pl.ANY)
    soil, head, sub, reach = pl.pallas_call(
        functools.partial(kernel, n),
        out_shape=(
            pltpu.VMEM(precip.shape, f32),
            pltpu.VMEM(head_init.shape, f32),
            pltpu.VMEM(head_init.shape, f32),
            pltpu.VMEM((slots // LANES, LANES), f32),
        ),
        in_specs=[anywhere] * 13,
        out_specs=(pl.BlockSpec(memory_space=pltpu.VMEM),) * 4,
        scratch_shapes=[
            pltpu.VMEM((4, cols, land_rows), f32),
            pltpu.VMEM((cols, land_rows), i32),
            pltpu.VMEM((LANES, land_rows), f32),
            pltpu.VMEM((n, land_dev, LANES), f32),
            pltpu.VMEM((per_chunk, chunks, land_dev, LANES), f32),
            pltpu.VMEM((chunks * land_dev, 4 * LANES), f32),
            tall,
            tall,
            tall,
            tall,
            pltpu.VMEM((full, width), i32),
            tall,
            tall,
            tall,
            tall,
            tall,
            tall,
            own,
            pltpu.VMEM((rows, width), i32),
            own,
            own,
            own,
            own,
            pltpu.VMEM((n, 1, LANES), f32),
            pltpu.VMEM((n, 1, LANES), f32),
            pltpu.VMEM((n, 1, LANES), i32),
            pltpu.VMEM((LANES, n * LANES), jnp.bfloat16),
            pltpu.SemaphoreType.DMA((5,)),
            pltpu.SemaphoreType.DMA((8,)),
            pltpu.SemaphoreType.DMA((2, 5)),
            pltpu.SemaphoreType.DMA((2, 5)),
            pltpu.SemaphoreType.DMA((3, n)),
            pltpu.SemaphoreType.DMA((3, n)),
        ],
        compiler_params=pltpu.CompilerParams(collective_id=0, has_side_effects=True, vmem_limit_bytes=16 * 2**20),
        name="step",
    )(*[pltpu.with_memory_space_constraint(x, pltpu.HBM) for x in (*args[:12], slot_reach.reshape(slots // LANES, 1, LANES))])
    results = (soil, head, sub, reach)
    soil, head, sub, reach = pl.pallas_call(
        flush,
        out_shape=tuple(jax.ShapeDtypeStruct(x.shape, x.dtype) for x in results),
        in_specs=[pl.BlockSpec(memory_space=pltpu.VMEM)] * 4,
        out_specs=(anywhere,) * 4,
        scratch_shapes=[pltpu.SemaphoreType.DMA((4,))],
        compiler_params=pltpu.CompilerParams(vmem_limit_bytes=2**20),
        name="flush",
    )(*results)
    return soil, head, sub, reach.reshape(slots)


def solution(mesh):
    grid = P(("member", "tile"), None)
    line = P(("member", "tile"))
    return jax.shard_map(
        local,
        mesh=mesh,
        in_specs=(grid,) * 12 + (line,),
        out_specs=(grid, grid, grid, line),
        check_vma=False,
    )
```
